32 devices in a mesh: box: 4 (over y, x), col: 8 (over z, core).
Axes of the slice: x: 2, y: 2, z: 4, core: 2. Of those that a mesh axis runs over, the one named last changes fastest.
Arguments:
- box_maps: bfloat16 [4, 2, 1024, 2048], P('box', None, 'col'), may hold values from -1 to 1
- group_loads: float32 [4, 128, 2048], P('box', 'col'), may hold values from -6 to 6
Outputs:
- top_maps: float32 [4, 2, 1024, 512], P('box', None, 'col')
- leaf_data: float32 [4, 512, 2048], P('box', 'col')
The draws below stay inside these ranges and needn't reach their ends.
All inputs are finite; a program needn't handle non-finite values.
Results may differ from the reference program's by a relative error of at most 0.0076.
Values may be sent and summed in bfloat16 or wider, within the bound.
No kernel may reach another device: no remote copies, remote signals or barrier semaphores. Data moves between devices by JAX's collectives and lax.ppermute only.
A program may use at most 192 MiB of HBM per device.

```python
import math
import jax
import jax.numpy as jnp

M = 2048
NLOAD = 512
BOXES = 4
LQ = 16
N_COL = 8


def invert_order(order):
    middle = order.shape[0]
    return jnp.zeros((middle,), jnp.int32).at[order].set(jnp.arange(middle, dtype=jnp.int32))


def draw_box_maps(key, part):
    middle = M // 2
    key_list = jax.random.split(key, 3)
    order_keys = jax.random.split(key_list[0], BOXES * 3)
    orders = jax.vmap(lambda sub_key: jax.random.permutation(sub_key, middle))(order_keys).reshape(BOXES, 3, middle).astype(jnp.int32)
    sign_ints = jax.random.randint(key_list[1], (BOXES, 3, middle), 0, 2).astype(jnp.int32) * 2 - 1
    first_order = orders[:, 0]
    second_order = orders[:, 1]
    third_order = orders[:, 2]
    first_sign = sign_ints[:, 0]
    second_sign = sign_ints[:, 1]
    third_sign = sign_ints[:, 2]
    inverse_first = jax.vmap(invert_order)(first_order)
    between_order = jnp.take_along_axis(second_order, inverse_first, axis=1)
    between_sign = jnp.take_along_axis(first_sign, inverse_first, axis=1) * jnp.take_along_axis(second_sign, inverse_first, axis=1)
    fourth_order = jnp.take_along_axis(between_order, third_order, axis=1)
    fourth_sign = third_sign * jnp.take_along_axis(between_sign, third_order, axis=1)
    all_orders = jnp.stack([first_order, third_order, second_order, fourth_order], axis=1).reshape(BOXES, 2, 2, middle)
    all_signs = jnp.stack([first_sign, third_sign, second_sign, fourth_sign], axis=1).reshape(BOXES, 2, 2, middle).astype(jnp.float32)
    matches = (all_orders[..., None, :] == jnp.arange(middle, dtype=jnp.int32)[:, None]).astype(jnp.float32)
    jitter = jax.random.normal(key_list[2], (BOXES, 2, 2, middle, middle), jnp.float32)
    scale_all = 0.9
    alpha = 0.97
    jitter_size = 0.03
    beta = math.sqrt(1.0 - alpha * alpha)
    weights = jnp.array([[alpha, beta], [beta, -alpha]], jnp.float32)
    coefficients = scale_all * weights[None, :, :, None, None] * all_signs[..., None, :]
    entries = coefficients * matches + jitter_size / math.sqrt(middle) * jitter
    return entries.transpose(0, 1, 3, 2, 4).reshape(BOXES, 2, middle, M).astype(jnp.bfloat16)


def shard_levels(key, extent, cuts, low, high):
    factor_of, own = 1.0, jax.random.fold_in(key, 6)
    for position, parts in cuts:
        draws = jnp.exp(jax.random.uniform(jax.random.fold_in(own, position), (parts,), jnp.float32, low / len(cuts), high / len(cuts)))
        factor_of = factor_of * jnp.repeat(draws, extent[position] // parts).reshape([-1 if axis == position else 1 for axis in range(len(extent))])
    return factor_of


def scatter_about(key, extent, scale, bound, shards=(), kind=jnp.bfloat16):
    values = jax.random.normal(key, extent, jnp.float32) * scale
    if len(shards) > 0:
        values = shard_levels(key, extent, shards, -0.22, 0.18) * values
    return jnp.clip(values, min=-bound, max=bound).astype(kind)


def setup_inputs(seed: int = 0) -> dict:
    seeds = jax.random.split(jax.random.key(seed), 3)
    return {
        "box_maps": draw_box_maps(jax.random.fold_in(seeds[2], 71), 0),
        "group_loads": scatter_about(seeds[1], (BOXES, NLOAD // 4, M), 1.0, 6.0, ((0, 4), (1, 8)), jnp.float32),
    }


def full_map(columns):
    return jnp.concatenate([columns[0], columns[1]], axis=0).T

def blocks(square):
    middle = square.shape[0] // 2
    return (square[:middle, :middle], square[:middle, middle:], square[middle:, :middle], square[middle:, middle:])

def factor(left_map, right_map):
    middle = left_map.shape[0] // 2
    product = jnp.dot(left_map[middle:, middle:].astype(jnp.float32), right_map[middle:, middle:].astype(jnp.float32), preferred_element_type=jnp.float32)
    return jnp.eye(middle, dtype=jnp.float32) - product

def merge_maps(left_map, right_map, coupling):
    left_outer, left_across, left_cross, left_inner = blocks(left_map)
    right_outer, right_across, right_cross, right_inner = blocks(right_map)
    solved_left = jnp.linalg.solve(coupling, left_cross.astype(jnp.float32)).astype(jnp.bfloat16)
    carried_left = jnp.dot(right_inner.astype(jnp.float32), solved_left.astype(jnp.float32), preferred_element_type=jnp.float32)
    upper_left = left_outer.astype(jnp.float32) + jnp.dot(left_across.astype(jnp.float32), carried_left.astype(jnp.bfloat16).astype(jnp.float32), preferred_element_type=jnp.float32)
    lower_left = jnp.dot(right_across.astype(jnp.float32), solved_left.astype(jnp.float32), preferred_element_type=jnp.float32)
    driven = jnp.dot(left_inner.astype(jnp.float32), right_cross.astype(jnp.float32), preferred_element_type=jnp.float32)
    solved_right = jnp.linalg.solve(coupling, driven).astype(jnp.bfloat16)
    carried_right = right_cross.astype(jnp.float32) + jnp.dot(right_inner.astype(jnp.float32), solved_right.astype(jnp.float32), preferred_element_type=jnp.float32)
    upper_right = jnp.dot(left_across.astype(jnp.float32), carried_right.astype(jnp.bfloat16).astype(jnp.float32), preferred_element_type=jnp.float32)
    lower_right = right_outer.astype(jnp.float32) + jnp.dot(right_across.astype(jnp.float32), solved_right.astype(jnp.float32), preferred_element_type=jnp.float32)
    return jnp.block([[upper_left, upper_right], [lower_left, lower_right]])

def descend(left_map, right_map, coupling, incoming):
    middle = left_map.shape[0] // 2
    left_cross = blocks(left_map)[2]
    left_inner = blocks(left_map)[3]
    right_cross = blocks(right_map)[2]
    right_inner = blocks(right_map)[3]
    given_left = incoming[:middle]
    given_right = incoming[middle:]
    through = jnp.dot(right_cross.astype(jnp.float32), given_right.astype(jnp.bfloat16).astype(jnp.float32), preferred_element_type=jnp.float32)
    driven = jnp.dot(left_cross.astype(jnp.float32), given_left.astype(jnp.bfloat16).astype(jnp.float32), preferred_element_type=jnp.float32) + jnp.dot(left_inner.astype(jnp.float32), through.astype(jnp.bfloat16).astype(jnp.float32), preferred_element_type=jnp.float32)
    solved_left = jnp.linalg.solve(coupling, driven)
    solved_right = through + jnp.dot(right_inner.astype(jnp.float32), solved_left.astype(jnp.bfloat16).astype(jnp.float32), preferred_element_type=jnp.float32)
    return (jnp.concatenate([given_left, solved_right], axis=0), jnp.concatenate([given_right, solved_left], axis=0))

def reference(box_maps, group_loads):
    boxes = box_maps.shape[0]
    ports = box_maps.shape[3]
    quarter = ports // 4
    top_list = []
    leaf_list = []
    for group_index in range(boxes // 4):
        box_list = [full_map(box_maps[4 * group_index + member]) for member in range(4)]
        coupling_left = factor(box_list[0], box_list[1])
        coupling_right = factor(box_list[2], box_list[3])
        pair_maps = [merge_maps(box_list[0], box_list[1], coupling_left).astype(jnp.bfloat16), merge_maps(box_list[2], box_list[3], coupling_right).astype(jnp.bfloat16)]
        coupling_top = factor(pair_maps[0], pair_maps[1])
        merged = merge_maps(pair_maps[0], pair_maps[1], coupling_top)
        columns = merged.T.reshape(2, ports // 2, 4, quarter).transpose(2, 0, 1, 3)
        top_list.append(columns)
        load_block = group_loads[4 * group_index:4 * group_index + 4]
        incoming = load_block.reshape(4, N_COL, LQ, ports).transpose(1, 0, 2, 3).reshape(NLOAD, ports).T
        left_in, right_in = descend(pair_maps[0], pair_maps[1], coupling_top, incoming)
        box_zero, box_one = descend(box_list[0], box_list[1], coupling_left, left_in)
        box_two, box_three = descend(box_list[2], box_list[3], coupling_right, right_in)
        leaf_list.extend([box_zero.T, box_one.T, box_two.T, box_three.T])
    return (jnp.concatenate(top_list, axis=0), jnp.stack(leaf_list))
```

```python
import functools
import jax
import jax.numpy as jnp
from jax import lax
from jax.experimental import pallas as pl
from jax.experimental.pallas import tpu as pltpu
from jax.sharding import Mesh, PartitionSpec as P

BF = jnp.bfloat16
F32 = jnp.float32
VMEM_LIMIT = 60 * 1024 * 1024
SMALL_POWER = 36.0
LAST_POWER = 1e12
MAX_SQUARINGS = 10
TARGET = 3e-5
MAX_STEPS = 12
MAX_NEWTON = 80


def mul(left, right):
    return jnp.dot(left, right, preferred_element_type=F32)


def mul_full(left, right):
    return jnp.dot(left, right, preferred_element_type=F32, precision=lax.Precision.HIGHEST)


def fold(values):
    rows, columns = values.shape
    return jnp.sum((values * values).reshape(rows // 8, 8, columns), axis=0)


def eye_block(start, rows, columns):
    row = lax.broadcasted_iota(jnp.int32, (rows, columns), 0) + start
    column = lax.broadcasted_iota(jnp.int32, (rows, columns), 1)
    return (row == column).astype(F32)


def factor_kernel(left, right, g_hi, g_lo, inverse, good, powers):
    middle = left.shape[0]
    block = min(256, middle)
    count = middle // block
    nothing = jnp.zeros((8, middle), F32)

    def first(index, total):
        rows = pl.ds(pl.multiple_of(index * block, block), block)
        product = mul(right[rows, :], left[...])
        high = product.astype(BF)
        g_hi[rows, :] = high
        powers[0, rows, :] = high
        g_lo[rows, :] = (product - high.astype(F32)).astype(BF)
        inverse[rows, :] = (product + eye_block(index * block, block, middle)).astype(BF)
        return total + fold(product)

    size = jnp.sum(lax.fori_loop(0, count, first, nothing))

    def more(state):
        step, size = state
        return (step < MAX_SQUARINGS) & (size >= SMALL_POWER) & (size < LAST_POWER)

    def double(state):
        step, _ = state
        now = lax.rem(step, 2)
        later = 1 - now

        def square(index, total):
            rows = pl.ds(pl.multiple_of(index * block, block), block)
            product = mul(powers[now, rows, :], powers[now])
            powers[later, rows, :] = product.astype(BF)
            return total + fold(product)

        size = jnp.sum(lax.fori_loop(0, count, square, nothing))

        def extend(index, carry):
            rows = pl.ds(pl.multiple_of(index * block, block), block)
            held = inverse[rows, :]
            inverse[rows, :] = (held.astype(F32) + mul(held, powers[later])).astype(BF)
            return carry

        lax.fori_loop(0, count, extend, 0)
        return (step + 1, size)

    _, size = lax.while_loop(more, double, (0, size))
    good[0] = (size < SMALL_POWER).astype(jnp.int32)


def factor(left, right):
    middle = left.shape[0]
    whole = jax.ShapeDtypeStruct((middle, middle), BF)
    inside = pl.BlockSpec(memory_space=pltpu.VMEM)
    return pl.pallas_call(
        factor_kernel,
        name="factor",
        out_shape=(whole, whole, whole, jax.ShapeDtypeStruct((1,), jnp.int32)),
        in_specs=[inside, inside],
        out_specs=(inside, inside, inside, pl.BlockSpec(memory_space=pltpu.SMEM)),
        scratch_shapes=[pltpu.VMEM((2, middle, middle), BF)],
        compiler_params=pltpu.CompilerParams(vmem_limit_bytes=VMEM_LIMIT),
    )(left, right)


def row_sums(values):
    return jnp.sum(values * values, axis=1, keepdims=True)


def refine(rhs, answer, g_hi, g_lo, inverse, good):
    answer[...] = mul(rhs[...].astype(BF), inverse[...])
    base = row_sums(rhs[...])
    base = jnp.where(base > 0, base, 1.0)

    def more(state):
        step, _, going = state
        return going == 1

    def correct(state):
        step, before, _ = state
        held = answer[...]
        high = held.astype(BF)
        low = (held - high.astype(F32)).astype(BF)
        rest = rhs[...] - held + mul(high, g_hi[...]) + (mul(low, g_hi[...]) + mul(high, g_lo[...]))
        answer[...] = held + mul(rest.astype(BF), inverse[...])
        now = jnp.max(row_sums(rest) / base)
        done = now * now <= (TARGET * TARGET) * before
        fails = jnp.logical_not(now < 0.25 * before) | (step >= MAX_STEPS)
        going = jnp.where(done, 0, jnp.where(fails, 2, 1)).astype(jnp.int32)
        return (step + 1, now, going)

    start = jnp.where(good[0] == 1, 1, 2).astype(jnp.int32)
    _, _, end = lax.while_loop(more, correct, (0, jnp.float32(1.0), start))
    return end


def general_solve(rhs, answer, left, right, square, rest, held):
    middle = left.shape[0]
    block = min(128, middle)
    wide = min(256, middle)
    count = middle // block

    def rows_of(index):
        return pl.ds(pl.multiple_of(index * block, block), block)

    def columns_of(index):
        return pl.ds(pl.multiple_of(index * wide, wide), wide)

    def build(index, total):
        rows = rows_of(index)
        values = eye_block(index * block, block, middle) - mul(right[rows, :], left[...])
        square[rows, :] = values
        size = jnp.abs(values)
        return (
            total[0] + jnp.sum(size, axis=0, keepdims=True),
            jnp.maximum(total[1], jnp.max(jnp.sum(size, axis=1, keepdims=True))),
        )

    column_total, row_most = lax.fori_loop(
        0, count, build, (jnp.zeros((1, middle), F32), jnp.float32(0.0))
    )
    scale = 1.0 / (jnp.max(column_total) * row_most)

    def turn(index, carry):
        row = pl.multiple_of(lax.div(index, count) * block, block)
        column = pl.multiple_of(lax.rem(index, count) * block, block)
        piece = square[pl.ds(row, block), pl.ds(column, block)]
        held[0, pl.ds(column, block), pl.ds(row, block)] = piece.T * scale
        return carry

    lax.fori_loop(0, count * count, turn, 0)
    wides = middle // wide

    def newton(state):
        step, _, before, _ = state
        now = lax.rem(step, 2)

        def residual(index, total):
            row = pl.multiple_of(lax.div(index, wides) * block, block)
            column = pl.multiple_of(lax.rem(index, wides) * wide, wide)
            rows, columns = pl.ds(row, block), pl.ds(column, wide)
            row_id = lax.broadcasted_iota(jnp.int32, (block, wide), 0) + row
            column_id = lax.broadcasted_iota(jnp.int32, (block, wide), 1) + column
            values = (row_id == column_id).astype(F32) - mul_full(
                held[now, rows, :], square[:, columns]
            )
            rest[rows, columns] = values
            return total + fold(values)

        size = jnp.sum(lax.fori_loop(0, count * wides, residual, jnp.zeros((8, wide), F32)))

        def update(index, carry):
            row = pl.multiple_of(lax.div(index, wides) * block, block)
            column = pl.multiple_of(lax.rem(index, wides) * wide, wide)
            rows, columns = pl.ds(row, block), pl.ds(column, wide)
            held[1 - now, rows, columns] = held[now, rows, columns] + mul_full(
                rest[rows, :], held[now, :, columns]
            )
            return carry

        lax.fori_loop(0, count * wides, update, 0)
        near = (size < 1e-5) | ((size < 0.1) & (size > 0.5 * before))
        return (step + 1, 1 - now, size, near.astype(jnp.int32))

    def more(state):
        step, _, _, near = state
        return (near == 0) & (step < MAX_NEWTON)

    _, now, _, _ = lax.while_loop(more, newton, (0, 0, jnp.float32(jnp.inf), 0))

    def by_columns(index, carry):
        columns = columns_of(index)
        answer[:, columns] = mul_full(rhs[...], held[now, :, columns])
        return carry

    lax.fori_loop(0, wides, by_columns, 0)
    count_rows = rhs.shape[0]

    def again(step, carry):
        def left_over(index, carry):
            columns = columns_of(index)
            rest[:count_rows, columns] = rhs[:, columns] - mul_full(answer[...], square[:, columns])
            return carry

        lax.fori_loop(0, wides, left_over, 0)

        def add(index, carry):
            columns = columns_of(index)
            answer[:, columns] += mul_full(rest[:count_rows, :], held[now, :, columns])
            return carry

        lax.fori_loop(0, wides, add, 0)
        return carry

    lax.fori_loop(0, 2, again, 0)


def apply_kernel(own, down, *refs):
    inputs = 6 + (2 if own else 0) + (3 if down else 0)
    outputs = (2 if own else 0) + (2 if down else 0)
    g_hi, g_lo, inverse, good, left, right = refs[:6]
    own_refs = refs[6:8] if own else ()
    down_refs = refs[inputs - 3 : inputs] if down else ()
    out_refs = refs[inputs : inputs + outputs]
    rhs, answer, through, square, rest, held = refs[inputs + outputs :]
    middle = left.shape[0]
    if own:
        left_own, right_own = own_refs
        rhs[:own, :] = left_own[...].astype(F32)
        rhs[own : 2 * own, :] = mul(right_own[...], left[...])
    if down:
        left_io, right_io, loads = down_refs
        passed = mul(loads[:, middle:].astype(BF), right_io[...])
        through[...] = passed
        rhs[2 * own :, :] = mul(loads[:, :middle].astype(BF), left_io[...]) + mul(
            passed.astype(BF), left[...]
        )
    end = refine(rhs, answer, g_hi, g_lo, inverse, good)

    @pl.when(end != 0)
    def _():
        general_solve(rhs, answer, left, right, square, rest, held)

    solved = answer[...].astype(BF)
    carried = mul(solved, right[...])
    if own:
        out_refs[0][...] = solved[: 2 * own]
        out_refs[1][:own, :] = carried[:own].astype(BF)
        out_refs[1][own:, :] = (right_own[...].astype(F32) + carried[own : 2 * own]).astype(BF)
    if down:
        out_refs[-2][...] = answer[2 * own :, :]
        out_refs[-1][...] = through[...] + carried[2 * own :]


def apply(factors, left, right, own_rows, down_rows):
    middle = left.shape[0]
    own = own_rows[0].shape[0] if own_rows else 0
    down = down_rows[2].shape[0] if down_rows else 0
    total = 2 * own + down
    inside = pl.BlockSpec(memory_space=pltpu.VMEM)
    out_shape = ()
    if own:
        out_shape += (jax.ShapeDtypeStruct((2 * own, middle), BF),) * 2
    if down:
        out_shape += (jax.ShapeDtypeStruct((down, middle), F32),) * 2
    arguments = (*factors, left, right, *own_rows, *down_rows)
    in_specs = [inside] * len(arguments)
    in_specs[3] = pl.BlockSpec(memory_space=pltpu.SMEM)
    return pl.pallas_call(
        functools.partial(apply_kernel, own, down),
        name="apply",
        out_shape=out_shape,
        in_specs=in_specs,
        out_specs=(inside,) * len(out_shape),
        scratch_shapes=[
            pltpu.VMEM((total, middle), F32),
            pltpu.VMEM((total, middle), F32),
            pltpu.VMEM((max(down, 8), middle), F32),
            pltpu.VMEM((middle, middle), F32),
            pltpu.VMEM((middle, middle), F32),
            pltpu.VMEM((2, middle, middle), F32),
        ],
        compiler_params=pltpu.CompilerParams(vmem_limit_bytes=VMEM_LIMIT),
    )(*arguments)


def gather(value, axes):
    return lax.all_gather(value, axes, axis=0, tiled=True)


def per_device(box_maps, group_loads):
    block = box_maps[0]
    own, ports = block.shape[1], block.shape[2]
    middle = ports // 2
    half = middle // 2
    low = lax.axis_index("lo")
    high = lax.axis_index("hi")
    position = lax.axis_index("col")
    is_left = low == 0
    pair = ("lo", "col")
    group = ("hi", "lo", "col")

    faces = gather(block[1][:, middle:], pair)
    left_ii, right_ii = faces[:middle], faces[middle:]
    mine = low * half
    other = half - mine

    def cut(side, start):
        return lax.dynamic_slice_in_dim(block[side], start, half, 1)

    cross = block[0][:, middle:]
    kept = jnp.concatenate([cut(0, mine), cross, cut(1, mine)], axis=1)
    sent = jnp.concatenate([cut(0, other), cross, cut(1, other)], axis=1)
    received = lax.ppermute(sent, "lo", [(0, 1), (1, 0)])
    left_all = jnp.where(is_left, kept, received)
    right_all = jnp.where(is_left, received, kept)
    outer = jnp.concatenate([left_all[:, half + middle :], right_all[:, half + middle :]], axis=1)
    outer = gather(outer, "col")
    loads = gather(group_loads[0], ("hi", "lo"))

    factors = factor(left_ii, right_ii)
    solved, carried = apply(
        factors,
        left_ii,
        right_ii,
        (left_all[:, half : half + middle], right_all[:, half : half + middle]),
        (),
    )
    upper = mul(carried, outer[:, :half])
    lower = mul(solved, outer[:, half:])
    upper_left = (left_all[:, :half].astype(F32) + upper[:own]).astype(BF)
    upper_right = upper[own:].astype(BF)
    lower_left = lower[:own].astype(BF)
    lower_right = (right_all[:, :half].astype(F32) + lower[own:]).astype(BF)

    def joined(value):
        whole = gather(value, group).reshape(2, 2, middle, half)
        return (
            jnp.concatenate([whole[0, 0], whole[0, 1]], axis=1),
            jnp.concatenate([whole[1, 0], whole[1, 1]], axis=1),
        )

    pair_left_ii, pair_right_ii = joined(lower_right)
    pair_left_io, pair_right_io = joined(lower_left)
    pair_outer = gather(upper_right, "col")
    cross_all = gather(cross, pair)

    pair_factors = factor(pair_left_ii, pair_right_ii)

    def own_rows(value):
        return lax.dynamic_slice_in_dim(value, position * own, own, 0)

    solved_two, carried_two, x_left, x_right = apply(
        pair_factors,
        pair_left_ii,
        pair_right_ii,
        (own_rows(pair_left_io), own_rows(pair_right_io)),
        (pair_left_io, pair_right_io, loads),
    )
    is_upper = high == 0
    top = mul(jnp.where(is_upper, carried_two, solved_two), pair_outer)
    outer_own = upper_left.astype(F32)
    nothing = jnp.zeros_like(outer_own)
    top = top + jnp.concatenate(
        [jnp.where(is_upper, outer_own, nothing), jnp.where(is_upper, nothing, outer_own)], axis=0
    )
    top_block = top.reshape(1, 2, own, half)

    first = jnp.where(is_upper, loads[:, :middle], loads[:, middle:])
    second = jnp.where(is_upper, x_right, x_left)
    pair_loads = jnp.concatenate([first, second], axis=1)
    y_left, y_right = apply(
        factors, left_ii, right_ii, (), (cross_all[:middle], cross_all[middle:], pair_loads)
    )
    leaf = jnp.concatenate(
        [jnp.where(is_left, first, second), jnp.where(is_left, y_right, y_left)], axis=1
    )
    return (top_block, leaf[None])


def solution(mesh):
    boxes, columns = mesh.devices.shape
    split = Mesh(mesh.devices.reshape(boxes // 4, 2, 2, columns), ("group", "hi", "lo", "col"))
    box = ("group", "hi", "lo")
    placed = (P(box, None, "col", None), P(box, "col", None))
    return jax.shard_map(
        per_device,
        mesh=split,
        in_specs=placed,
        out_specs=placed,
        check_vma=False,
    )
```

```python
import functools
import jax
import jax.numpy as jnp
from jax import lax
from jax.experimental import pallas as pl
from jax.experimental.pallas import tpu as pltpu
from jax.sharding import Mesh, PartitionSpec as P

BF = jnp.bfloat16
F32 = jnp.float32
VMEM_LIMIT = 60 * 1024 * 1024
SMALL_POWER = 36.0
LAST_POWER = 1e12
MAX_SQUARINGS = 10
TARGET = 3e-5
MAX_STEPS = 12
MAX_NEWTON = 80


def mul(left, right):
    return jnp.dot(left, right, preferred_element_type=F32)


def mul_full(left, right):
    return jnp.dot(left, right, preferred_element_type=F32, precision=lax.Precision.HIGHEST)


def fold(values):
    rows, columns = values.shape
    return jnp.sum((values * values).reshape(rows // 8, 8, columns), axis=0)


def eye_block(start, rows, columns):
    row = lax.broadcasted_iota(jnp.int32, (rows, columns), 0) + start
    column = lax.broadcasted_iota(jnp.int32, (rows, columns), 1)
    return (row == column).astype(F32)


def coordinates():
    return lax.axis_index("hi"), lax.axis_index("lo"), lax.axis_index("col")


def origin(step):
    hops, low_even, low_odd, high_even, high_odd, crossed = step
    high, low, column = coordinates()
    size = lax.axis_size("col")
    core = lax.rem(column, 2)
    core = 1 - core if crossed else core
    row = lax.rem(lax.div(column, 2) + size // 2 - hops, size // 2) * 2 + core
    flip_low = low_even + (low_odd - low_even) * core
    flip_high = high_even + (high_odd - high_even) * core
    return high + flip_high - 2 * high * flip_high, low + flip_low - 2 * low * flip_low, row


def place(layout, step, target, own):
    high, low, row = origin(step)
    rows = pl.ds(pl.multiple_of(row * own, own), own)
    if layout == "pair":
        return target.at[low, rows, :]
    if layout == "group":
        width = target.shape[2] // 2
        return target.at[high, rows, pl.ds(pl.multiple_of(low * width, width), width)]
    return target.at[rows, :]


def fetch(layout, steps, own, parts, target, arrived):
    copies = []
    for part, inner in zip(parts, steps):
        for index, step in enumerate(inner):
            copy = pltpu.make_async_copy(
                part.at[pl.ds(index * own, own), :],
                place(layout, step, target, own),
                arrived.at[len(copies)],
            )
            copy.start()
            copies.append(copy)
    return copies


def count_blocks(steps):
    return sum(len(inner) for inner in steps)


def factor_kernel(layout, steps, own, *refs):
    parts = refs[: len(steps)]
    faces, g_hi, g_lo, inverse, good, powers, arrived = refs[len(steps) :]
    middle = faces.shape[1]
    for copy in fetch(layout, steps, own, parts, faces, arrived):
        copy.wait()
    product = mul(faces[1], faces[0])
    high = product.astype(BF)
    g_hi[...] = high
    powers[0] = high
    g_lo[...] = (product - high.astype(F32)).astype(BF)
    inverse[...] = (product + eye_block(0, middle, middle)).astype(BF)
    size = jnp.sum(fold(product))

    def more(state):
        step, size = state
        return (step < MAX_SQUARINGS) & (size >= SMALL_POWER) & (size < LAST_POWER)

    def double(state):
        step, _ = state
        now = lax.rem(step, 2)
        later = 1 - now
        product = mul(powers[now], powers[now])
        powers[later] = product.astype(BF)
        size = jnp.sum(fold(product))
        held = inverse[...]
        inverse[...] = (held.astype(F32) + mul(held, powers[later])).astype(BF)
        return (step + 1, size)

    _, size = lax.while_loop(more, double, (0, size))
    good[0] = (size < SMALL_POWER).astype(jnp.int32)


INSIDE = pl.BlockSpec(memory_space=pltpu.VMEM)
OUTSIDE = pl.BlockSpec(memory_space=pl.ANY)
SCALAR = pl.BlockSpec(memory_space=pltpu.SMEM)


def factor(layout, parts, steps, own):
    middle = lax.axis_size("col") * own
    whole = jax.ShapeDtypeStruct((middle, middle), BF)
    faces = jax.ShapeDtypeStruct((2, middle, middle), BF)
    return pl.pallas_call(
        functools.partial(factor_kernel, layout, steps, own),
        name="factor",
        out_shape=(faces, whole, whole, whole, jax.ShapeDtypeStruct((1,), jnp.int32)),
        in_specs=[OUTSIDE] * len(parts),
        out_specs=(INSIDE, INSIDE, INSIDE, INSIDE, SCALAR),
        scratch_shapes=[
            pltpu.VMEM((2, middle, middle), BF),
            pltpu.SemaphoreType.DMA((count_blocks(steps),)),
        ],
        compiler_params=pltpu.CompilerParams(vmem_limit_bytes=VMEM_LIMIT),
    )(*parts)


def row_sums(values):
    return jnp.sum(values * values, axis=1, keepdims=True)


def refine(rhs, answer, rest, g_hi, g_lo, inverse, good):
    base = row_sums(rhs[...])
    base = jnp.where(base > 0, base, 1.0)

    def advance(now):
        part = mul(now.astype(BF), inverse[...]).astype(BF)
        left_over = now - part.astype(F32) + (mul(part, g_hi[...]) + mul(part, g_lo[...]))
        rest[...] = left_over
        return part.astype(F32), jnp.max(row_sums(left_over) / base)

    part, size = advance(rhs[...])
    answer[...] = part

    def judge(step, before, now):
        done = now * now <= (TARGET * TARGET) * before
        fails = jnp.logical_not(now < 0.25 * before) | (step >= MAX_STEPS)
        return jnp.where(done, 0, jnp.where(fails, 2, 1)).astype(jnp.int32)

    def more(state):
        return state[2] == 1

    def correct(state):
        step, before, _ = state
        part, now = advance(rest[...])
        answer[...] += part
        return (step + 1, now, judge(step + 1, before, now))

    first = judge(0, jnp.float32(1.0), size)
    start = jnp.where(good[0] == 1, first, 2).astype(jnp.int32)
    _, _, end = lax.while_loop(more, correct, (0, size, start))
    answer[...] += mul(rest[...].astype(BF), inverse[...])
    return end


def general_solve(rhs, answer, left, right, square, rest, held):
    middle = left.shape[0]
    block = min(128, middle)
    wide = min(256, middle)
    count = middle // block

    def rows_of(index):
        return pl.ds(pl.multiple_of(index * block, block), block)

    def columns_of(index):
        return pl.ds(pl.multiple_of(index * wide, wide), wide)

    def build(index, total):
        rows = rows_of(index)
        values = eye_block(index * block, block, middle) - mul(right[rows, :], left[...])
        square[rows, :] = values
        size = jnp.abs(values)
        return (
            total[0] + jnp.sum(size, axis=0, keepdims=True),
            jnp.maximum(total[1], jnp.max(jnp.sum(size, axis=1, keepdims=True))),
        )

    column_total, row_most = lax.fori_loop(
        0, count, build, (jnp.zeros((1, middle), F32), jnp.float32(0.0))
    )
    scale = 1.0 / (jnp.max(column_total) * row_most)

    def turn(index, carry):
        row = pl.multiple_of(lax.div(index, count) * block, block)
        column = pl.multiple_of(lax.rem(index, count) * block, block)
        piece = square[pl.ds(row, block), pl.ds(column, block)]
        held[0, pl.ds(column, block), pl.ds(row, block)] = piece.T * scale
        return carry

    lax.fori_loop(0, count * count, turn, 0)
    wides = middle // wide

    def newton(state):
        step, _, before, _ = state
        now = lax.rem(step, 2)

        def residual(index, total):
            row = pl.multiple_of(lax.div(index, wides) * block, block)
            column = pl.multiple_of(lax.rem(index, wides) * wide, wide)
            rows, columns = pl.ds(row, block), pl.ds(column, wide)
            row_id = lax.broadcasted_iota(jnp.int32, (block, wide), 0) + row
            column_id = lax.broadcasted_iota(jnp.int32, (block, wide), 1) + column
            values = (row_id == column_id).astype(F32) - mul_full(
                held[now, rows, :], square[:, columns]
            )
            rest[rows, columns] = values
            return total + fold(values)

        size = jnp.sum(lax.fori_loop(0, count * wides, residual, jnp.zeros((8, wide), F32)))

        def update(index, carry):
            row = pl.multiple_of(lax.div(index, wides) * block, block)
            column = pl.multiple_of(lax.rem(index, wides) * wide, wide)
            rows, columns = pl.ds(row, block), pl.ds(column, wide)
            held[1 - now, rows, columns] = held[now, rows, columns] + mul_full(
                rest[rows, :], held[now, :, columns]
            )
            return carry

        lax.fori_loop(0, count * wides, update, 0)
        near = (size < 1e-5) | ((size < 0.1) & (size > 0.5 * before))
        return (step + 1, 1 - now, size, near.astype(jnp.int32))

    def more(state):
        step, _, _, near = state
        return (near == 0) & (step < MAX_NEWTON)

    _, now, _, _ = lax.while_loop(more, newton, (0, 0, jnp.float32(jnp.inf), 0))

    def by_columns(index, carry):
        columns = columns_of(index)
        answer[:, columns] = mul_full(rhs[...], held[now, :, columns])
        return carry

    lax.fori_loop(0, wides, by_columns, 0)
    count_rows = rhs.shape[0]

    def again(step, carry):
        def left_over(index, carry):
            columns = columns_of(index)
            rest[:count_rows, columns] = rhs[:, columns] - mul_full(answer[...], square[:, columns])
            return carry

        lax.fori_loop(0, wides, left_over, 0)

        def add(index, carry):
            columns = columns_of(index)
            answer[:, columns] += mul_full(rest[:count_rows, :], held[now, :, columns])
            return carry

        lax.fori_loop(0, wides, add, 0)
        return carry

    lax.fori_loop(0, 2, again, 0)


def apply_kernel(own, down, layout, steps, choice, *refs):
    inputs = 5 + (2 if own and not down else 0) + (1 + len(steps) if down else 0)
    outputs = (2 if own else 0) + (1 if down else 0)
    faces, g_hi, g_lo, inverse, good = refs[:5]
    out_refs = refs[inputs : inputs + outputs]
    rhs, answer, through, square, rest, held, cross, arrived = refs[inputs + outputs :]
    left, right = faces.at[0], faces.at[1]
    middle = left.shape[0]
    high, low, column = coordinates()
    if down:
        loads = refs[5]
        block = middle // lax.axis_size("col")
        for copy in fetch(layout, steps, block, refs[6:inputs], cross, arrived):
            copy.wait()
        if own:
            rows = pl.ds(pl.multiple_of(column * own, own), own)
            left_own, right_own = cross[0, rows, :], cross[1, rows, :]
    else:
        kept, received = refs[5][...], refs[6][...]
        left_own = jnp.where(low == 0, kept, received)
        right_own = jnp.where(low == 0, received, kept)
    if own:
        rhs[:own, :] = left_own.astype(F32)
        rhs[own : 2 * own, :] = mul(right_own, left[...])
    if down:
        passed = mul(loads[:, middle:].astype(BF), cross[1])
        through[...] = passed
        rhs[2 * own :, :] = mul(loads[:, :middle].astype(BF), cross[0]) + mul(
            passed.astype(BF), left[...]
        )
    end = refine(rhs, answer, rest.at[: rhs.shape[0]], g_hi, g_lo, inverse, good)

    @pl.when(end != 0)
    def _():
        general_solve(rhs, answer, left, right, square, rest, held)

    solved = answer[...].astype(BF)
    carried = mul(solved, right[...])
    if own:
        out_refs[0][...] = solved[: 2 * own]
        out_refs[1][:own, :] = carried[:own].astype(BF)
        out_refs[1][own:, :] = (right_own.astype(F32) + carried[own : 2 * own]).astype(BF)
    if down:
        first = (high if choice == "hi" else low) == 0
        result = out_refs[-1]
        result[:, :middle] = jnp.where(first, loads[:, :middle], loads[:, middle:])
        result[:, middle:] = jnp.where(
            first, through[...] + carried[2 * own :], answer[2 * own :, :]
        )


def apply(factors, own, own_rows, layout, parts, steps, loads, choice):
    middle = factors[0].shape[1]
    down = 0 if loads is None else loads.shape[0]
    total = 2 * own + down
    out_shape = ()
    if own:
        out_shape += (jax.ShapeDtypeStruct((2 * own, middle), BF),) * 2
    if down:
        out_shape += (jax.ShapeDtypeStruct((down, 2 * middle), F32),)
    arguments = (*factors, *own_rows, *((loads,) if down else ()), *parts)
    in_specs = [INSIDE] * 4 + [SCALAR] + [INSIDE] * (len(own_rows) + (1 if down else 0))
    in_specs += [OUTSIDE] * len(parts)
    return pl.pallas_call(
        functools.partial(apply_kernel, own, down, layout, steps, choice),
        name="apply",
        out_shape=out_shape,
        in_specs=in_specs,
        out_specs=(INSIDE,) * len(out_shape),
        scratch_shapes=[
            pltpu.VMEM((total, middle), F32),
            pltpu.VMEM((total, middle), F32),
            pltpu.VMEM((max(down, 8), middle), F32),
            pltpu.VMEM((middle, middle), F32),
            pltpu.VMEM((middle, middle), F32),
            pltpu.VMEM((2, middle, middle), F32),
            pltpu.VMEM((2, middle, middle) if down else (2, 16, middle), BF),
            pltpu.SemaphoreType.DMA((max(count_blocks(steps), 1),)),
        ],
        compiler_params=pltpu.CompilerParams(vmem_limit_bytes=VMEM_LIMIT),
    )(*arguments)


def merge_kernel(steps, own, *refs):
    parts = refs[4 : 4 + len(steps)]
    solved, carried, kept, received = refs[:4]
    upper_left, upper_right, lower_left, lower_right, outer, arrived = refs[4 + len(steps) :]
    half = upper_left.shape[1]
    _, low, _ = coordinates()
    for copy in fetch("col", steps, own, parts, outer, arrived):
        copy.wait()
    at_left = pl.ds(pl.multiple_of(low * half, half), half)
    at_right = pl.ds(pl.multiple_of((1 - low) * half, half), half)
    upper = mul(carried[...], outer[:, at_left])
    lower = mul(solved[...], outer[:, at_right])
    one, two = kept[:, :half].astype(F32), received[:, :half].astype(F32)
    upper_left[...] = (jnp.where(low == 0, one, two) + upper[:own]).astype(BF)
    upper_right[...] = upper[own:].astype(BF)
    lower_left[...] = lower[:own].astype(BF)
    lower_right[...] = (jnp.where(low == 0, two, one) + lower[own:]).astype(BF)


def merge(solved, carried, kept, received, parts, steps, own):
    middle = solved.shape[1]
    half = middle // 2
    return pl.pallas_call(
        functools.partial(merge_kernel, steps, own),
        name="merge",
        out_shape=(jax.ShapeDtypeStruct((own, half), BF),) * 4,
        in_specs=[INSIDE] * 4 + [OUTSIDE] * len(parts),
        out_specs=(INSIDE,) * 4,
        scratch_shapes=[
            pltpu.VMEM((middle, middle), BF),
            pltpu.SemaphoreType.DMA((count_blocks(steps),)),
        ],
        compiler_params=pltpu.CompilerParams(vmem_limit_bytes=VMEM_LIMIT),
    )(solved, carried, kept, received, *parts)


def top_kernel(steps, own, *refs):
    parts = refs[3 : 3 + len(steps)]
    solved, carried, outer_own = refs[:3]
    result, outer, arrived = refs[3 + len(steps) :]
    high, _, _ = coordinates()
    for copy in fetch("col", steps, own, parts, outer, arrived):
        copy.wait()
    is_upper = high == 0
    chosen = jnp.where(is_upper, carried[...], solved[...])
    product = mul(chosen, outer[...])
    added = outer_own[...].astype(F32)
    result[:own, :] = product[:own] + jnp.where(is_upper, added, 0.0)
    result[own:, :] = product[own:] + jnp.where(is_upper, 0.0, added)


def top_rows(solved, carried, outer_own, parts, steps, own):
    middle = solved.shape[1]
    half = outer_own.shape[1]
    return pl.pallas_call(
        functools.partial(top_kernel, steps, own),
        name="top",
        out_shape=jax.ShapeDtypeStruct((2 * own, half), F32),
        in_specs=[INSIDE] * 3 + [OUTSIDE] * len(parts),
        out_specs=INSIDE,
        scratch_shapes=[
            pltpu.VMEM((middle, half), BF),
            pltpu.SemaphoreType.DMA((count_blocks(steps),)),
        ],
        compiler_params=pltpu.CompilerParams(vmem_limit_bytes=VMEM_LIMIT),
    )(solved, carried, outer_own, *parts)


def along_z(value, hops):
    size = lax.axis_size("col")
    return lax.ppermute(value, "col", [(i, (i + 2 * hops) % size) for i in range(size)])


def across_core(value):
    size = lax.axis_size("col")
    return lax.ppermute(value, "col", [(i, i ^ 1) for i in range(size)])


def across(value, axis):
    return lax.ppermute(value, axis, [(0, 1), (1, 0)])


def across_by_core(value, even_low):
    size = lax.axis_size("col")
    pairs = []
    for source in range(4 * size):
        box, column = divmod(source, size)
        flip = 1 if (column % 2 == 0) == even_low else 2
        pairs.append((source, (box ^ flip) * size + column))
    return lax.ppermute(value, ("hi", "lo", "col"), pairs)


def hop_list():
    return range(1, lax.axis_size("col") // 2)


def with_cores(parts, steps):
    crossed = [across_core(part) for part in parts]
    swapped = tuple(tuple((*step[:5], 1) for step in inner) for inner in steps)
    return (*parts, *crossed), (*steps, *swapped)


def gather_column(value):
    parts = [value, *(along_z(value, hops) for hops in hop_list())]
    steps = tuple(((hops, 0, 0, 0, 0, 0),) for hops in range(len(parts)))
    return with_cores(parts, steps)


def gather_pair(value, swapped=None):
    parts = [value, *(along_z(value, hops) for hops in hop_list())]
    steps = tuple(((hops, 0, 0, 0, 0, 0),) for hops in range(len(parts)))
    others = [across(part, "lo") for part in parts] if swapped is None else [
        swapped,
        *(across(part, "lo") for part in parts[1:]),
    ]
    more = tuple(((hops, 1, 1, 0, 0, 0),) for hops in range(len(parts)))
    return with_cores((*parts, *others), (*steps, *more))


def gather_group(value):
    pieces = [value, *(along_z(value, hops) for hops in hop_list())]
    stack = jnp.concatenate(pieces, axis=0)
    one = across_by_core(stack, True)
    two = across_by_core(stack, False)
    both = across_by_core(one, False)
    flips = ((0, 0, 0, 0), (1, 0, 0, 1), (0, 1, 1, 0), (1, 1, 1, 1))
    steps = tuple(tuple((hops, *flip, 0) for hops in range(len(pieces))) for flip in flips)
    return with_cores((stack, one, two, both), steps)


def per_device(box_maps, group_loads):
    block = box_maps[0]
    own, ports = block.shape[1], block.shape[2]
    middle = ports // 2
    half = middle // 2
    low = lax.axis_index("lo")
    mine = low * half
    other = half - mine

    def cut(start):
        return jnp.concatenate(
            [lax.dynamic_slice_in_dim(block[side], start, half, 1) for side in range(2)], axis=1
        )

    inner_parts, inner_steps = gather_pair(block[1][:, middle:])
    kept = cut(mine)
    received = across(cut(other), "lo")
    outer_parts, outer_steps = gather_column(
        jnp.concatenate([kept[:, half:], received[:, half:]], axis=1)
    )
    cross = block[0][:, middle:]
    cross_other = across(cross, "lo")
    cross_parts, cross_steps = gather_pair(cross, cross_other)
    near = across(group_loads[0], "lo")
    both = jnp.where(
        low == 0,
        jnp.concatenate([group_loads[0], near], axis=0),
        jnp.concatenate([near, group_loads[0]], axis=0),
    )
    far = across(both, "hi")
    loads = jnp.where(
        lax.axis_index("hi") == 0,
        jnp.concatenate([both, far], axis=0),
        jnp.concatenate([far, both], axis=0),
    )

    factors = factor("pair", inner_parts, inner_steps, own)
    solved, carried = apply(factors, own, (cross, cross_other), "pair", (), (), None, "lo")
    upper_left, upper_right, lower_left, lower_right = merge(
        solved, carried, kept, received, outer_parts, outer_steps, own
    )

    pair_inner_parts, pair_inner_steps = gather_group(lower_right)
    pair_cross_parts, pair_cross_steps = gather_group(lower_left)
    pair_outer_parts, pair_outer_steps = gather_column(upper_right)
    pair_factors = factor("group", pair_inner_parts, pair_inner_steps, own)
    solved_two, carried_two, pair_loads = apply(
        pair_factors, own, (), "group", pair_cross_parts, pair_cross_steps, loads, "hi"
    )
    top = top_rows(solved_two, carried_two, upper_left, pair_outer_parts, pair_outer_steps, own)
    (leaf,) = apply(factors, 0, (), "pair", cross_parts, cross_steps, pair_loads, "lo")
    return (top.reshape(1, 2, own, half), leaf[None])


def solution(mesh):
    boxes, columns = mesh.devices.shape
    split = Mesh(mesh.devices.reshape(boxes // 4, 2, 2, columns), ("group", "hi", "lo", "col"))
    box = ("group", "hi", "lo")
    placed = (P(box, None, "col", None), P(box, "col", None))
    return jax.shard_map(
        per_device,
        mesh=split,
        in_specs=placed,
        out_specs=placed,
        check_vma=False,
    )
```
